32 devices in a mesh: pair: 8 (over z, y), row: 4 (over x, core).
Axes of the slice: x: 2, y: 2, z: 4, core: 2. Of those that a mesh axis runs over, the one named last changes fastest.
Arguments:
- snapshots: float32 [1024, 16384], P('pair', 'row'), may hold values from -50 to 50
- live_rows: int32 [4], P('row'), may hold values from 2048 to 4096, as said below
Outputs:
- rotated: float32 [1024, 16384], P('pair', 'row')
The draws below stay inside these ranges and needn't reach their ends.
Inputs may be any that keep to these rules, and one draw needn't show every extreme that they name: Row slot s of row index r is live when s < live_rows[r]; every draw has a row index with all 4096 slots live.
All inputs are finite; a program needn't handle non-finite values.
Results may differ from the reference program's by a relative error of at most 0.0003.
Values sent between devices are 32-bit elements; how exact they have to be, the bound alone decides.
A program may use at most 64 MiB of HBM per device.

```python
import math
import jax
import jax.numpy as jnp
from jax import lax

ROWS_DEV = 4096
BLOCK = 64
ROUNDS = 4
NS_STEPS = 3
ROWS = 16384
COLS = 1024
N_PAIR = 8
N_ROW = 4


def draw_snapshots(key, part):
    key_list = jax.random.split(jax.random.fold_in(key, 3), 3)
    column_scale = jnp.exp(jax.random.uniform(key_list[0], (COLS, 1), jnp.float32, math.log(0.3), math.log(3.0)))
    row_scale = jnp.exp(jax.random.uniform(key_list[1], (1, ROWS), jnp.float32, math.log(0.3), math.log(3.0)))
    base = jnp.clip(jax.random.normal(key_list[2], (COLS, ROWS), jnp.float32), -4.0, 4.0)
    return base * column_scale * row_scale


def draw_live_rows(key, part):
    first_key, second_key = jax.random.split(jax.random.fold_in(key, 7))
    counts = jax.random.randint(first_key, (N_ROW,), ROWS_DEV // 2, ROWS_DEV + 1)
    full_index = jax.random.randint(second_key, (), 0, N_ROW)
    return jnp.where(jnp.arange(N_ROW) == full_index, ROWS_DEV, counts).astype(jnp.int32)


def setup_inputs(seed: int = 0) -> dict:
    arg_keys = jax.random.split(jax.random.key(seed), 3)
    snapshots = draw_snapshots(jax.random.fold_in(arg_keys[2], 71), 0)
    live_rows = draw_live_rows(jax.random.fold_in(arg_keys[2], 71), 0)
    return {"snapshots": snapshots, "live_rows": live_rows}


EPSILON = 1e-06
PRECISE = lax.Precision.HIGHEST

def make_rotation(cross_block, column_norms):
    block_width = cross_block.shape[0]
    upper_norm = column_norms[:block_width][:, None]
    lower_norm = column_norms[block_width:][None, :]
    spread = lower_norm - upper_norm
    coupling = cross_block * spread / (spread * spread + 4.0 * cross_block * cross_block + upper_norm * lower_norm + EPSILON)
    blank_block = jnp.zeros((block_width, block_width), jnp.float32)
    generator = jnp.concatenate([jnp.concatenate([blank_block, coupling], 1), jnp.concatenate([-coupling.T, blank_block], 1)], 0)
    damping = 1.0 / jnp.sqrt(1.0 + 2.0 * jnp.sum(coupling * coupling))
    rotation = (jnp.eye(2 * block_width, dtype=jnp.float32) + generator) * damping
    for iteration in range(NS_STEPS):
        product = jnp.dot(rotation.T, rotation, precision=PRECISE, preferred_element_type=jnp.float32)
        rotation = 1.5 * rotation - 0.5 * jnp.dot(rotation, product, precision=PRECISE, preferred_element_type=jnp.float32)
    return rotation

def pair_round(pair_block):
    gram_matrix = jnp.dot(pair_block, pair_block.T, precision=PRECISE, preferred_element_type=jnp.float32)
    rotation = make_rotation(gram_matrix[:BLOCK, BLOCK:], jnp.diagonal(gram_matrix))
    return jnp.dot(rotation.T, pair_block, precision=PRECISE, preferred_element_type=jnp.float32)

def reference(snapshots, live_rows):
    slot_index = jnp.arange(ROWS, dtype=jnp.int32)
    live_limit = jnp.repeat(live_rows, ROWS_DEV)
    masked = jnp.where((slot_index % ROWS_DEV < live_limit)[None, :], snapshots, jnp.zeros((), jnp.float32))
    pair_rows = masked.reshape(N_PAIR, 2 * BLOCK, ROWS)
    for round_index in range(ROUNDS):
        pair_rows = lax.map(pair_round, pair_rows)
        if round_index + 1 < ROUNDS:
            top_blocks = pair_rows[:, :BLOCK]
            bottom_blocks = pair_rows[:, BLOCK:]
            new_tops = jnp.concatenate([top_blocks[:1], bottom_blocks[:1], top_blocks[1:N_PAIR - 1]], 0)
            new_bottoms = jnp.concatenate([bottom_blocks[1:], top_blocks[N_PAIR - 1:]], 0)
            pair_rows = jnp.concatenate([new_tops, new_bottoms], 1)
    return pair_rows.reshape(2 * BLOCK * N_PAIR, ROWS)
```

```python
import functools

import jax
import jax.numpy as jnp
from jax import lax
from jax.experimental import pallas as pl
from jax.experimental.pallas import tpu as pltpu
from jax.sharding import PartitionSpec as P

NS_STEPS = 3
EPSILON = 1e-06
MESH = pl.DeviceIdType.MESH
CHUNKS = 8
EARLY = 2
AHEAD = 4
HELD_BACK = 3


def own_product(block):
    high, low = halves(block)
    dims = (((1,), (1,)), ((), ()))
    return lax.dot_general(
        jnp.concatenate([high, high], 1),
        jnp.concatenate([high, low], 1),
        dims,
        preferred_element_type=jnp.float32,
    ) + lax.dot_general(low, high, dims, preferred_element_type=jnp.float32)


def eye_mask(rows, columns):
    row = lax.broadcasted_iota(jnp.int32, (rows, columns), 0)
    column = lax.broadcasted_iota(jnp.int32, (rows, columns), 1)
    return row == column


def halves(block):
    high = block.astype(jnp.bfloat16)
    return high, (block - high.astype(jnp.float32)).astype(jnp.bfloat16)


def gram_parts(block):
    high, low = halves(block)
    return lax.dot_general(
        high,
        jnp.concatenate([high, low], 0),
        (((1,), (1,)), ((), ())),
        preferred_element_type=jnp.float32,
    )


def gram_of(parts):
    full = parts.shape[0]
    mixed = parts[:, full:]
    return parts[:, :full] + mixed + mixed.T


def turn_halves(turn):
    high, low = halves(turn)
    return jnp.concatenate([high, high], 1), low


def turned(turn, block):
    wide, low_turn = turn
    high, low = halves(block)
    return jnp.dot(
        wide, jnp.concatenate([high, low], 0), preferred_element_type=jnp.float32
    ) + jnp.dot(low_turn, high, preferred_element_type=jnp.float32)


def norms_of(gram):
    return jnp.sum(jnp.where(eye_mask(*gram.shape), gram, 0.0), axis=0, keepdims=True)


def pack_two(first, second, width):
    lane = lax.broadcasted_iota(jnp.int32, (width, 2 * width), 1)
    line = lax.broadcasted_iota(jnp.int32, (8, 2 * width), 0)
    cross = jnp.where(lane < width, pltpu.roll(second[:width], width, 1), first[:width])
    return cross, jnp.where(line == 0, norms_of(first), norms_of(second))


def pack_one(gram, width):
    part = width // 2
    lane = lax.broadcasted_iota(jnp.int32, (part, 2 * width), 1)
    cross = jnp.where(lane < width, pltpu.roll(gram[:part], width, 1), gram[part:width])
    return cross, jnp.broadcast_to(norms_of(gram), (8, 2 * width))


def rotation_transposed(cross, norms, width):
    full = 2 * width
    lane = lax.broadcasted_iota(jnp.int32, (width, full), 1)
    cross = jnp.where(lane >= width, cross, 0.0)
    upper = jnp.sum(jnp.where(eye_mask(width, full), norms, 0.0), axis=1, keepdims=True)
    spread = norms - upper
    coupling = cross * spread / (spread * spread + 4.0 * cross * cross + upper * norms + EPSILON)
    squares = jnp.sum(jnp.sum(coupling * coupling, axis=1, keepdims=True), axis=0, keepdims=True)
    damping = 1.0 / jnp.sqrt(1.0 + 2.0 * squares)
    corner = jnp.concatenate([coupling, jnp.zeros((width, full), jnp.float32)], 0)
    identity = jnp.where(eye_mask(full, full), 1.0, 0.0)
    return (identity - corner + corner.T) * damping


def orthogonalised(turns):
    for _ in range(NS_STEPS):
        products = [own_product(t) for t in turns]
        turns = [1.5 * t - 0.5 * turned(turn_halves(g), t) for t, g in zip(turns, products)]
    return turns


def kernel(
    pairs, rows, stop, live_ref, x_hbm, out_ref, x_ref, raw, state1, state2, state3, raw2, final,
    singles, doubles, triples, packed, load_sem, raw_send, raw_recv, fwd_sem,
    one_send, one_recv, two_send, two_recv, three_send, three_recv,
    move_send, move_recv, raw2_send, raw2_recv, last_send, last_recv,
):
    p, r = lax.axis_index("pair"), lax.axis_index("row")
    plane, y = p // 2, p % 2
    last_plane = pairs // 2 - 1
    partner = 2 * plane + 1 - y
    me = y * rows + r
    full, cells = x_ref.shape
    width = full // 2
    part = width // 2
    half = cells // 2
    step = half // CHUNKS
    first, last = plane == 0, plane == last_plane
    pending = []

    def plane_device(other):
        return 2 * plane + other // rows, lax.rem(other, rows)

    barrier = pltpu.get_barrier_semaphore()
    for k in range(1, 2 * rows):
        pl.semaphore_signal(
            barrier, inc=1, device_id=plane_device(lax.rem(me + k, 2 * rows)), device_id_type=MESH
        )

    @pl.when(jnp.logical_not(first))
    def _():
        pl.semaphore_signal(barrier, inc=1, device_id=(p - 2, r), device_id_type=MESH)

    @pl.when(jnp.logical_not(last))
    def _():
        pl.semaphore_signal(barrier, inc=1, device_id=(p + 2, r), device_id_type=MESH)

    def columns(h, c):
        return pl.ds(pl.multiple_of(h * half + c * step, step), step)

    def load(k):
        span = pl.ds(2 * k * step, 2 * step)
        return pltpu.make_async_copy(x_hbm.at[:, span], x_ref.at[:, span], load_sem.at[k])

    for k in range(CHUNKS):
        load(k).start()

    def remote(source, target, send_sem, recv_sem, pair_to, row_to=r):
        return pltpu.make_async_remote_copy(
            src_ref=source,
            dst_ref=target,
            send_sem=send_sem,
            recv_sem=recv_sem,
            device_id=(pair_to, row_to),
            device_id_type=MESH,
        )

    def arrived(target, recv_sem):
        pltpu.make_async_copy(target, target, recv_sem).wait()

    def raw_copy(c):
        return remote(x_hbm.at[:, columns(1 - y, c)], raw.at[c], raw_send.at[c], raw_recv.at[c], partner)

    def raw_start(c):
        raw_copy(c).start()
        pending.append(lambda: raw_copy(c).wait_send())

    def sum_of(buffer, count):
        result = buffer[0]
        for k in range(1, count):
            result = result + buffer[k]
        return result

    live = live_ref[0]

    def masked(block, start, size):
        slot = lax.broadcasted_iota(jnp.int32, (1, size), 1) + start
        return jnp.where(slot < live, block, 0.0)

    def place(which, side):
        if which == 0:
            return jnp.where(first, 0, 2) if side == 0 else jnp.where(first, 2, 5)
        return jnp.where(last, 3, 4) if side == 0 else 1

    def up(number, state, c):
        return remote(
            state.at[4, c], state.at[0, c], move_send.at[number, 0, c], move_recv.at[number, 0, c], p + 2
        )

    def down(number, state, c):
        return remote(
            state.at[5, c], state.at[3, c], move_send.at[number, 1, c], move_recv.at[number, 1, c], p - 2
        )

    def place_turned(number, state, which, turn, block, c):
        result = turned(turn, block)
        if which == 0:
            state[place(0, 0), c] = result[:width]
            state[place(0, 1), c] = result[width:]

            @pl.when(jnp.logical_not(first))
            def _():
                down(number, state, c).start()
        else:
            state[place(1, 0), c] = result[:width]
            state[place(1, 1), c] = result[width:]

            @pl.when(jnp.logical_not(last))
            def _():
                up(number, state, c).start()

    def finish_moves(number, state):
        for c in range(CHUNKS):
            @pl.when(jnp.logical_not(first))
            def _():
                down(number, state, c).wait_send()

            @pl.when(jnp.logical_not(last))
            def _():
                up(number, state, c).wait_send()

    def wait_moved(number, state, c):
        @pl.when(jnp.logical_not(first))
        def _():
            arrived(state.at[0, c], move_recv.at[number, 0, c])

        @pl.when(jnp.logical_not(last))
        def _():
            arrived(state.at[3, c], move_recv.at[number, 1, c])

    def pair_block(state, which, c):
        return state[pl.ds(2 * which, 2), c].reshape(full, step)

    def turn_of(result):
        cross = jnp.concatenate([pltpu.roll(result[:part], width, 1), result[:part]], 0)
        return rotation_transposed(cross, result[part : part + 1], width)

    def turn_two(number, grams):
        cross, tail = pack_two(grams[0], grams[1], width)
        doubles[number, me, pl.ds(0, width)] = cross
        doubles[number, me, pl.ds(width, 8)] = tail
        copies = []
        for k in range(1, 2 * rows):
            copy = remote(
                doubles.at[number, me],
                doubles.at[number, me],
                two_send.at[number, k],
                two_recv.at[number, k],
                *plane_device(lax.rem(me + k, 2 * rows)),
            )
            copy.start()
            copies.append(copy)
        for copy in copies:
            copy.wait_recv()
        pending.append(lambda: [copy.wait_send() for copy in copies])
        result = sum_of(doubles.at[number], 2 * rows)
        return orthogonalised([
            rotation_transposed(result[:width], result[width : width + 1], width),
            rotation_transposed(pltpu.roll(result[:width], width, 1), result[width + 1 : width + 2], width),
        ])

    def finish():
        for wait in pending:
            wait()

    parts = jnp.zeros((full, 2 * full), jnp.float32)
    near = jnp.where(first, 0, 1) + jnp.where(last, 0, 1)
    for k in range(CHUNKS):
        if k == CHUNKS // 2:
            pl.semaphore_wait(barrier, 2 * rows - 1 + near)
            for c in range(EARLY):
                raw_start(c)
        load(k).wait()
        span = pl.ds(2 * k * step, 2 * step)
        parts = parts + gram_parts(masked(x_ref[:, span], 2 * k * step, 2 * step))
    cross, tail = pack_one(gram_of(parts), width)
    singles[r, pl.ds(0, part)] = cross
    singles[r, pl.ds(part, 8)] = tail
    one_copies = []
    for k in range(1, rows):
        copy = remote(singles.at[r], singles.at[r], one_send.at[k], one_recv.at[k], p, lax.rem(r + k, rows))
        copy.start()
        one_copies.append(copy)
    for copy in one_copies:
        copy.wait_recv()
    pending.append(lambda: [copy.wait_send() for copy in one_copies])
    result = sum_of(singles, rows)
    packed[0] = result
    forward = remote(packed.at[0], packed.at[1], fwd_sem.at[0], fwd_sem.at[1], partner)
    forward.start()
    for c in range(EARLY, CHUNKS):
        raw_start(c)
    own = turn_halves(orthogonalised([turn_of(result)])[0])

    def round_zero(turn, mine, c):
        block = x_ref[:, columns(y, c)] if mine else raw[c]
        block = masked(block, y * half + c * step, step)
        for number in range(2):
            @pl.when((y if mine else 1 - y) == number)
            def _():
                place_turned(0, state1, number, turn, block, c)

    for c in range(CHUNKS):
        round_zero(own, True, c)
    forward.wait_recv()
    pending.append(lambda: forward.wait_send())
    other = turn_halves(orthogonalised([turn_of(packed[1])])[0])
    for c in range(CHUNKS):
        raw_copy(c).wait_recv()
        round_zero(other, False, c)

    moves = [(0, c) for c in range(CHUNKS)]
    pending.append(lambda: finish_moves(0, state1))
    if stop == 1:
        for c in range(CHUNKS):
            wait_moved(0, state1, c)
        out_ref[0:64, 0:step] = state1[0, 0]
        return finish()

    parts = [jnp.zeros((full, 2 * full), jnp.float32)] * 2
    for c in range(CHUNKS):
        wait_moved(0, state1, c)
        parts = [parts[which] + gram_parts(pair_block(state1, which, c)) for which in range(2)]
    turns = turn_two(0, [gram_of(q) for q in parts])
    if stop == 2:
        out_ref[0:128, 0:128] = turns[0] + turns[1]
        return finish()
    turns = [turn_halves(t) for t in turns]
    for c in range(CHUNKS):
        for which in range(2):
            place_turned(1, state2, which, turns[which], pair_block(state1, which, c), c)
    pending.append(lambda: finish_moves(1, state2))

    def raw2_copy(c):
        return remote(state2.at[pl.ds(2 * y, 2), c], raw2.at[c], raw2_send.at[c], raw2_recv.at[c], partner)

    parts = [jnp.zeros((full, 2 * full), jnp.float32)] * 2
    for c in range(CHUNKS):
        wait_moved(1, state2, c)
        if c < AHEAD:
            raw2_copy(c).start()
        parts = [parts[which] + gram_parts(pair_block(state2, which, c)) for which in range(2)]
    pending.append(lambda: [raw2_copy(c).wait_send() for c in range(AHEAD)])
    if stop == 3:
        for c in range(AHEAD):
            raw2_copy(c).wait_recv()
        out_ref[0:128, 0:256] = parts[0] + parts[1]
        return finish()
    turns = turn_two(1, [gram_of(q) for q in parts])
    if stop == 4:
        for c in range(AHEAD):
            raw2_copy(c).wait_recv()
        out_ref[0:128, 0:128] = turns[0] + turns[1]
        return finish()

    near_side = jnp.where(y == 0, 0, 1)
    near_slot = jnp.where(y == 0, 2, 1)
    far_slot = jnp.where(y == 0, 3, 0)

    def back_near(c):
        return remote(
            state3.at[near_slot, c], final.at[near_side, c], last_send.at[0, c], last_recv.at[0, c], partner
        )

    def back_far(c):
        return remote(
            state3.at[far_slot, c], final.at[1 - near_side, c], last_send.at[1, c], last_recv.at[1, c], partner
        )

    order = list(range(AHEAD, CHUNKS)) + list(range(AHEAD))
    halves_of = [turn_halves(t) for t in turns]
    for c in order:
        for which in range(2):
            place_turned(2, state3, which, halves_of[which], pair_block(state2, which, c), c)
        if c >= AHEAD:
            back_near(c).start()
    pending.append(lambda: finish_moves(2, state3))
    pending.append(lambda: [back_near(c).wait_send() for c in range(AHEAD, CHUNKS)])

    even_rows = jnp.where(first, turns[0][width:], turns[0][:width])
    taken = turn_halves(jnp.where(y == 1, even_rows, turns[1][width:]))
    for c in range(AHEAD):
        raw2_copy(c).wait_recv()
        final[1 - near_side, c] = turned(taken, raw2[c].reshape(full, step))

    parts = [jnp.zeros((full, 2 * full), jnp.float32)] * 2
    for n, c in enumerate(order):
        wait_moved(2, state3, c)
        if n < CHUNKS - HELD_BACK:
            back_far(c).start()
        parts = [parts[which] + gram_parts(pair_block(state3, which, c)) for which in range(2)]
    if stop == 5:
        out_ref[0:128, 0:256] = parts[0] + parts[1]
        for n, c in enumerate(order):
            if n < CHUNKS - HELD_BACK:
                back_far(c).wait()
        for c in range(AHEAD, CHUNKS):
            back_near(c).wait_recv()
        return finish()
    for which in range(2):
        cross, tail = pack_one(gram_of(parts[which]), width)
        packed[2 + which, pl.ds(0, part)] = cross
        packed[2 + which, pl.ds(part, 8)] = tail

        @pl.when(y == which)
        def _():
            triples[me, pl.ds(0, part)] = cross
            triples[me, pl.ds(part, 8)] = tail

    three_copies = []
    for k in range(1, 2 * rows):
        other_me = lax.rem(me + k, 2 * rows)
        copy = remote(
            packed.at[2 + other_me // rows], triples.at[me], three_send.at[k], three_recv.at[k],
            *plane_device(other_me),
        )
        copy.start()
        three_copies.append(copy)
    for n, c in enumerate(order):
        if n >= CHUNKS - HELD_BACK:
            back_far(c).start()
    pending.append(lambda: [back_far(c).wait_send() for c in range(CHUNKS)])
    for copy in three_copies:
        copy.wait_recv()
    pending.append(lambda: [copy.wait_send() for copy in three_copies])
    own = turn_halves(orthogonalised([turn_of(sum_of(triples, 2 * rows))])[0])
    if stop == 6:
        out_ref[0:128, 0:256] = own[0].astype(jnp.float32)
        for c in range(CHUNKS):
            back_far(c).wait_recv()
        for c in range(AHEAD, CHUNKS):
            back_near(c).wait_recv()
        return finish()
    for c in order:
        out_ref[:, columns(y, c)] = turned(own, pair_block(state3, y, c))
    for c in order:
        if c >= AHEAD:
            back_near(c).wait_recv()
        back_far(c).wait_recv()
        out_ref[:, columns(1 - y, c)] = turned(own, final[:, c].reshape(full, step))
    finish()


def solution(mesh, stop=0):
    pairs, rows = mesh.shape["pair"], mesh.shape["row"]

    def body(snapshots, live_rows):
        full, cells = snapshots.shape
        width, half = full // 2, cells // 2
        step = half // CHUNKS
        state = pltpu.VMEM((6, CHUNKS, width, step), jnp.float32)
        copies = pltpu.SemaphoreType.DMA
        return pl.pallas_call(
            functools.partial(kernel, pairs, rows, stop),
            out_shape=jax.ShapeDtypeStruct(snapshots.shape, jnp.float32),
            in_specs=[
                pl.BlockSpec(memory_space=pltpu.SMEM),
                pl.BlockSpec(memory_space=pltpu.HBM),
            ],
            out_specs=pl.BlockSpec(memory_space=pltpu.VMEM),
            scratch_shapes=[
                pltpu.VMEM((full, cells), jnp.float32),
                pltpu.VMEM((CHUNKS, full, step), jnp.float32),
                state,
                state,
                state,
                pltpu.VMEM((AHEAD, 2, width, step), jnp.float32),
                pltpu.VMEM((2, CHUNKS, width, step), jnp.float32),
                pltpu.VMEM((rows, width // 2 + 8, full), jnp.float32),
                pltpu.VMEM((2, 2 * rows, width + 8, full), jnp.float32),
                pltpu.VMEM((2 * rows, width // 2 + 8, full), jnp.float32),
                pltpu.VMEM((4, width // 2 + 8, full), jnp.float32),
                copies((CHUNKS,)),
                copies((CHUNKS,)),
                copies((CHUNKS,)),
                copies((2,)),
                copies((rows,)),
                copies((rows,)),
                copies((2, 2 * rows)),
                copies((2, 2 * rows)),
                copies((2 * rows,)),
                copies((2 * rows,)),
                copies((3, 2, CHUNKS)),
                copies((3, 2, CHUNKS)),
                copies((AHEAD,)),
                copies((AHEAD,)),
                copies((2, CHUNKS)),
                copies((2, CHUNKS)),
            ],
            compiler_params=pltpu.CompilerParams(
                collective_id=0, has_side_effects=True, vmem_limit_bytes=48 * 1024 * 1024
            ),
        )(live_rows, snapshots)

    return jax.shard_map(
        body,
        mesh=mesh,
        in_specs=(P("pair", "row"), P("row")),
        out_specs=P("pair", "row"),
        check_vma=False,
    )
```

```python
import functools

import jax
import jax.numpy as jnp
from jax import lax
from jax.experimental import pallas as pl
from jax.experimental.pallas import tpu as pltpu
from jax.sharding import PartitionSpec as P

NS_STEPS = 3
EPSILON = 1e-06
MESH = pl.DeviceIdType.MESH
CHUNKS = 8
EARLY = 2
AHEAD = 3
AHEAD_FIRST = 2
RAW_ONE = 4
RAW_TWO = 2
RAW_AFTER = (3, 5, 7, 7)
BACK_FIRST = 4


def own_product(block):
    high, low = halves(block)
    dims = (((1,), (1,)), ((), ()))
    return lax.dot_general(
        jnp.concatenate([high, high], 1),
        jnp.concatenate([high, low], 1),
        dims,
        preferred_element_type=jnp.float32,
    ) + lax.dot_general(low, high, dims, preferred_element_type=jnp.float32)


def eye_mask(rows, columns):
    row = lax.broadcasted_iota(jnp.int32, (rows, columns), 0)
    column = lax.broadcasted_iota(jnp.int32, (rows, columns), 1)
    return row == column


def halves(block):
    high = block.astype(jnp.bfloat16)
    return high, (block - high.astype(jnp.float32)).astype(jnp.bfloat16)


def gram_parts(block):
    high, low = halves(block)
    return lax.dot_general(
        high,
        jnp.concatenate([high, low], 0),
        (((1,), (1,)), ((), ())),
        preferred_element_type=jnp.float32,
    )


def gram_of(parts):
    full = parts.shape[0]
    mixed = parts[:, full:]
    return parts[:, :full] + mixed + mixed.T


def turn_halves(turn):
    high, low = halves(turn)
    return jnp.concatenate([high, high], 1), low


def turned(turn, block):
    wide, low_turn = turn
    high, low = halves(block)
    return jnp.dot(
        wide, jnp.concatenate([high, low], 0), preferred_element_type=jnp.float32
    ) + jnp.dot(low_turn, high, preferred_element_type=jnp.float32)


def norms_of(gram):
    return jnp.sum(jnp.where(eye_mask(*gram.shape), gram, 0.0), axis=0, keepdims=True)


def pack_two(first, second, width):
    lane = lax.broadcasted_iota(jnp.int32, (width, 2 * width), 1)
    line = lax.broadcasted_iota(jnp.int32, (8, 2 * width), 0)
    cross = jnp.where(lane < width, pltpu.roll(second[:width], width, 1), first[:width])
    return cross, jnp.where(line == 0, norms_of(first), norms_of(second))


def pack_one(gram, width):
    part = width // 2
    lane = lax.broadcasted_iota(jnp.int32, (part, 2 * width), 1)
    cross = jnp.where(lane < width, pltpu.roll(gram[:part], width, 1), gram[part:width])
    return cross, jnp.broadcast_to(norms_of(gram), (8, 2 * width))


def rotation_transposed(cross, norms, width):
    full = 2 * width
    lane = lax.broadcasted_iota(jnp.int32, (width, full), 1)
    cross = jnp.where(lane >= width, cross, 0.0)
    upper = jnp.sum(jnp.where(eye_mask(width, full), norms, 0.0), axis=1, keepdims=True)
    spread = norms - upper
    coupling = cross * spread / (spread * spread + 4.0 * cross * cross + upper * norms + EPSILON)
    squares = jnp.sum(jnp.sum(coupling * coupling, axis=1, keepdims=True), axis=0, keepdims=True)
    damping = 1.0 / jnp.sqrt(1.0 + 2.0 * squares)
    corner = jnp.concatenate([coupling, jnp.zeros((width, full), jnp.float32)], 0)
    identity = jnp.where(eye_mask(full, full), 1.0, 0.0)
    return (identity - corner + corner.T) * damping


def orthogonalised(turns):
    for _ in range(NS_STEPS):
        products = [own_product(t) for t in turns]
        turns = [1.5 * t - 0.5 * turned(turn_halves(g), t) for t, g in zip(turns, products)]
    return turns


def kernel(
    pairs, rows, live_ref, x_hbm, out_ref, x_ref, raw, state1, state2, state3, raw2, final, far1, far2, rows_out, rows_in,
    singles, doubles, triples, packed, load_sem, raw_send, raw_recv, fwd_sem,
    one_send, one_recv, two_send, two_recv, three_send, three_recv,
    move_send, move_recv, raw2_send, raw2_recv, last_send, last_recv,
    far_send, far_recv, rows_send, rows_recv,
):
    p, r = lax.axis_index("pair"), lax.axis_index("row")
    plane, y = p // 2, p % 2
    last_plane = pairs // 2 - 1
    partner = 2 * plane + 1 - y
    me = y * rows + r
    full, cells = x_ref.shape
    width = full // 2
    part = width // 2
    half = cells // 2
    step = half // CHUNKS
    first, last = plane == 0, plane == last_plane
    pending = []

    def plane_device(other):
        return 2 * plane + other // rows, lax.rem(other, rows)

    barrier = pltpu.get_barrier_semaphore()
    for k in range(1, 2 * rows):
        pl.semaphore_signal(
            barrier, inc=1, device_id=plane_device(lax.rem(me + k, 2 * rows)), device_id_type=MESH
        )

    @pl.when(jnp.logical_not(first))
    def _():
        pl.semaphore_signal(barrier, inc=1, device_id=(p - 2, r), device_id_type=MESH)

    @pl.when(jnp.logical_not(last))
    def _():
        pl.semaphore_signal(barrier, inc=1, device_id=(p + 2, r), device_id_type=MESH)

    def columns(h, c):
        return pl.ds(pl.multiple_of(h * half + c * step, step), step)

    def load(k):
        span = pl.ds(2 * k * step, 2 * step)
        return pltpu.make_async_copy(x_hbm.at[:, span], x_ref.at[:, span], load_sem.at[k])

    for k in range(CHUNKS):
        load(k).start()

    def remote(source, target, send_sem, recv_sem, pair_to, row_to=r):
        return pltpu.make_async_remote_copy(
            src_ref=source,
            dst_ref=target,
            send_sem=send_sem,
            recv_sem=recv_sem,
            device_id=(pair_to, row_to),
            device_id_type=MESH,
        )

    def arrived(target, recv_sem):
        pltpu.make_async_copy(target, target, recv_sem).wait()

    def raw_copy(c):
        return remote(x_hbm.at[:, columns(1 - y, c)], raw.at[c], raw_send.at[c], raw_recv.at[c], partner)

    def raw_start(c):
        raw_copy(c).start()
        pending.append(lambda: raw_copy(c).wait_send())

    def sum_of(buffer, count):
        result = buffer[0]
        for k in range(1, count):
            result = result + buffer[k]
        return result

    live = live_ref[0]

    def masked(block, start, size):
        slot = lax.broadcasted_iota(jnp.int32, (1, size), 1) + start
        return jnp.where(slot < live, block, 0.0)

    def place(which, side):
        if which == 0:
            return jnp.where(first, 0, 2) if side == 0 else jnp.where(first, 2, 5)
        return jnp.where(last, 3, 4) if side == 0 else 1

    def up(number, state, c):
        return remote(
            state.at[4, c], state.at[0, c], move_send.at[number, 0, c], move_recv.at[number, 0, c], p + 2
        )

    def down(number, state, c):
        return remote(
            state.at[5, c], state.at[3, c], move_send.at[number, 1, c], move_recv.at[number, 1, c], p - 2
        )

    def place_turned(number, state, which, turn, block, c, send=True):
        result = turned(turn, block)
        if which == 0:
            state[place(0, 0), c] = result[:width]
            state[place(0, 1), c] = result[width:]
            if send:
                @pl.when(jnp.logical_not(first))
                def _():
                    down(number, state, c).start()
        else:
            state[place(1, 0), c] = result[:width]
            state[place(1, 1), c] = result[width:]
            if send:
                @pl.when(jnp.logical_not(last))
                def _():
                    up(number, state, c).start()

    def far_copies(number, state, c):
        buffer = (far1, far2)[number]
        lower = remote(
            state.at[pl.ds(0, 2), c], buffer.at[0, c], far_send.at[number, 0, c], far_recv.at[number, 0, c], p - 2
        )
        upper = remote(
            state.at[pl.ds(2, 2), c], buffer.at[1, c], far_send.at[number, 1, c], far_recv.at[number, 1, c], p + 2
        )
        return lower, upper

    def rows_copies(number):
        lower = remote(
            rows_out.at[number, 0], rows_in.at[number, 0], rows_send.at[number, 0], rows_recv.at[number, 0], p - 2
        )
        upper = remote(
            rows_out.at[number, 1], rows_in.at[number, 1], rows_send.at[number, 1], rows_recv.at[number, 1], p + 2
        )
        return lower, upper

    def both_ways(copies, action):
        @pl.when(jnp.logical_not(first))
        def _():
            getattr(copies[0], action)()

        @pl.when(jnp.logical_not(last))
        def _():
            getattr(copies[1], action)()

    def far_start(number, state, c):
        both_ways(far_copies(number, state, c), "start")
        pending.append(lambda: both_ways(far_copies(number, state, c), "wait_send"))

    def rows_start(number, turns):
        rows_out[number, 0] = turns[0][width:]
        rows_out[number, 1] = turns[1][:width]
        both_ways(rows_copies(number), "start")
        pending.append(lambda: both_ways(rows_copies(number), "wait_send"))

    def rows_wait(number):
        @pl.when(jnp.logical_not(last))
        def _():
            arrived(rows_in.at[number, 0], rows_recv.at[number, 0])

        @pl.when(jnp.logical_not(first))
        def _():
            arrived(rows_in.at[number, 1], rows_recv.at[number, 1])

    def far_turned(number, state, c):
        buffer = (far1, far2)[number]

        @pl.when(jnp.logical_not(last))
        def _():
            arrived(buffer.at[0, c], far_recv.at[number, 0, c])
            state[3, c] = turned(turn_halves(rows_in[number, 0]), buffer[0, c].reshape(full, step))

        @pl.when(jnp.logical_not(first))
        def _():
            arrived(buffer.at[1, c], far_recv.at[number, 1, c])
            state[0, c] = turned(turn_halves(rows_in[number, 1]), buffer[1, c].reshape(full, step))

    def finish_moves(number, state, start=0):
        for c in range(start, CHUNKS):
            @pl.when(jnp.logical_not(first))
            def _():
                down(number, state, c).wait_send()

            @pl.when(jnp.logical_not(last))
            def _():
                up(number, state, c).wait_send()

    def wait_moved(number, state, c):
        @pl.when(jnp.logical_not(first))
        def _():
            arrived(state.at[0, c], move_recv.at[number, 0, c])

        @pl.when(jnp.logical_not(last))
        def _():
            arrived(state.at[3, c], move_recv.at[number, 1, c])

    def pair_block(state, which, c):
        return state[pl.ds(2 * which, 2), c].reshape(full, step)

    def turn_of(result):
        cross = jnp.concatenate([pltpu.roll(result[:part], width, 1), result[:part]], 0)
        return rotation_transposed(cross, result[part : part + 1], width)

    def turn_two(number, grams, between=lambda: None):
        cross, tail = pack_two(grams[0], grams[1], width)
        doubles[number, me, pl.ds(0, width)] = cross
        doubles[number, me, pl.ds(width, 8)] = tail
        copies = []
        for k in range(1, 2 * rows):
            copy = remote(
                doubles.at[number, me],
                doubles.at[number, me],
                two_send.at[number, k],
                two_recv.at[number, k],
                *plane_device(lax.rem(me + k, 2 * rows)),
            )
            copy.start()
            copies.append(copy)
        between()
        for copy in copies:
            copy.wait_recv()
        pending.append(lambda: [copy.wait_send() for copy in copies])
        result = sum_of(doubles.at[number], 2 * rows)
        return orthogonalised([
            rotation_transposed(result[:width], result[width : width + 1], width),
            rotation_transposed(pltpu.roll(result[:width], width, 1), result[width + 1 : width + 2], width),
        ])

    def finish():
        for wait in pending:
            wait()

    parts = jnp.zeros((full, 2 * full), jnp.float32)
    near = jnp.where(first, 0, 1) + jnp.where(last, 0, 1)
    for k in range(CHUNKS):
        if k == CHUNKS // 2:
            pl.semaphore_wait(barrier, 2 * rows - 1 + near)
            for c in range(EARLY):
                raw_start(c)
        load(k).wait()
        span = pl.ds(2 * k * step, 2 * step)
        parts = parts + gram_parts(masked(x_ref[:, span], 2 * k * step, 2 * step))
    cross, tail = pack_one(gram_of(parts), width)
    singles[r, pl.ds(0, part)] = cross
    singles[r, pl.ds(part, 8)] = tail
    one_copies = []
    for k in range(1, rows):
        copy = remote(singles.at[r], singles.at[r], one_send.at[k], one_recv.at[k], p, lax.rem(r + k, rows))
        copy.start()
        one_copies.append(copy)
    for copy in one_copies:
        copy.wait_recv()
    pending.append(lambda: [copy.wait_send() for copy in one_copies])
    result = sum_of(singles, rows)
    packed[0] = result
    forward = remote(packed.at[0], packed.at[1], fwd_sem.at[0], fwd_sem.at[1], partner)
    forward.start()
    for c in range(EARLY, CHUNKS):
        raw_start(c)
    own = turn_halves(orthogonalised([turn_of(result)])[0])

    def round_zero(turn, mine, c):
        block = x_ref[:, columns(y, c)] if mine else raw[c]
        block = masked(block, y * half + c * step, step)
        for number in range(2):
            @pl.when((y if mine else 1 - y) == number)
            def _():
                place_turned(0, state1, number, turn, block, c)

    for c in range(CHUNKS):
        round_zero(own, True, c)
    forward.wait_recv()
    pending.append(lambda: forward.wait_send())
    other = turn_halves(orthogonalised([turn_of(packed[1])])[0])
    zero = jnp.zeros((full, 2 * full), jnp.float32)
    parts = [zero, zero]

    def add_gram(parts, state, c):
        return [parts[which] + gram_parts(pair_block(state, which, c)) for which in range(2)]

    for c in range(CHUNKS):
        raw_copy(c).wait_recv()
        round_zero(other, False, c)
        for j in range(RAW_ONE):
            if RAW_AFTER[j] == c:
                wait_moved(0, state1, j)
                far_start(0, state1, j)
                parts = add_gram(parts, state1, j)
    pending.append(lambda: finish_moves(0, state1))
    for c in range(RAW_ONE, CHUNKS):
        wait_moved(0, state1, c)
        parts = add_gram(parts, state1, c)
    turns = turn_two(0, [gram_of(q) for q in parts])
    rows_start(0, turns)
    turns = [turn_halves(t) for t in turns]
    for c in list(range(RAW_ONE, CHUNKS)) + list(range(RAW_ONE)):
        for which in range(2):
            place_turned(1, state2, which, turns[which], pair_block(state1, which, c), c, c >= RAW_ONE)
    pending.append(lambda: finish_moves(1, state2, RAW_ONE))

    def raw2_copy(c):
        return remote(state2.at[pl.ds(2 * y, 2), c], raw2.at[c], raw2_send.at[c], raw2_recv.at[c], partner)

    parts = [zero, zero]
    rows_wait(0)
    for c in range(CHUNKS):
        if c < RAW_ONE:
            far_turned(0, state2, c)
        else:
            wait_moved(1, state2, c)
        if c < AHEAD_FIRST:
            raw2_copy(c).start()
        if c < RAW_TWO:
            far_start(1, state2, c)
        parts = add_gram(parts, state2, c)

    def rest_ahead():
        for c in range(AHEAD_FIRST, AHEAD):
            raw2_copy(c).start()

    pending.append(lambda: [raw2_copy(c).wait_send() for c in range(AHEAD)])
    turns = turn_two(1, [gram_of(q) for q in parts], rest_ahead)
    near_side = jnp.where(y == 0, 0, 1)
    near_slot = jnp.where(y == 0, 2, 1)
    far_slot = jnp.where(y == 0, 3, 0)

    def back_near(c):
        return remote(
            state3.at[near_slot, c], final.at[near_side, c], last_send.at[0, c], last_recv.at[0, c], partner
        )

    def back_far(c):
        return remote(
            state3.at[far_slot, c], final.at[1 - near_side, c], last_send.at[1, c], last_recv.at[1, c], partner
        )

    rows_start(1, turns)
    halves_of = [turn_halves(t) for t in turns]
    order = [c for c in range(AHEAD, CHUNKS) if c >= RAW_TWO]
    order += [c for c in range(RAW_TWO, CHUNKS) if c not in order]
    order += [c for c in range(CHUNKS) if c not in order]
    for c in order:
        for which in range(2):
            place_turned(2, state3, which, halves_of[which], pair_block(state2, which, c), c, c >= RAW_TWO)
        if c >= AHEAD:
            back_near(c).start()
    pending.append(lambda: finish_moves(2, state3, RAW_TWO))
    pending.append(lambda: [back_near(c).wait_send() for c in range(AHEAD, CHUNKS)])

    parts = [zero, zero]
    order = list(range(RAW_TWO)) + [c for c in order if c >= RAW_TWO]
    rows_wait(1)
    for n, c in enumerate(order):
        if c < RAW_TWO:
            far_turned(1, state3, c)
        else:
            wait_moved(2, state3, c)
        if n < BACK_FIRST:
            back_far(c).start()
        parts = add_gram(parts, state3, c)
    for which in range(2):
        cross, tail = pack_one(gram_of(parts[which]), width)
        packed[2 + which, pl.ds(0, part)] = cross
        packed[2 + which, pl.ds(part, 8)] = tail

        @pl.when(y == which)
        def _():
            triples[me, pl.ds(0, part)] = cross
            triples[me, pl.ds(part, 8)] = tail

    three_copies = []
    for k in range(1, 2 * rows):
        other_me = lax.rem(me + k, 2 * rows)
        copy = remote(
            packed.at[2 + other_me // rows], triples.at[me], three_send.at[k], three_recv.at[k],
            *plane_device(other_me),
        )
        copy.start()
        three_copies.append(copy)
    for c in order[BACK_FIRST:]:
        back_far(c).start()
    even_rows = jnp.where(first, turns[0][width:], turns[0][:width])
    taken = turn_halves(jnp.where(y == 1, even_rows, turns[1][width:]))
    for c in range(AHEAD):
        raw2_copy(c).wait_recv()
        final[1 - near_side, c] = turned(taken, raw2[c].reshape(full, step))
    pending.append(lambda: [back_far(c).wait_send() for c in range(CHUNKS)])
    for copy in three_copies:
        copy.wait_recv()
    pending.append(lambda: [copy.wait_send() for copy in three_copies])
    own = turn_halves(orthogonalised([turn_of(sum_of(triples, 2 * rows))])[0])
    for c in order:
        out_ref[:, columns(y, c)] = turned(own, pair_block(state3, y, c))
    for c in order:
        if c >= AHEAD:
            back_near(c).wait_recv()
        back_far(c).wait_recv()
        out_ref[:, columns(1 - y, c)] = turned(own, final[:, c].reshape(full, step))
    finish()


def solution(mesh):
    pairs, rows = mesh.shape["pair"], mesh.shape["row"]

    def body(snapshots, live_rows):
        full, cells = snapshots.shape
        width, half = full // 2, cells // 2
        step = half // CHUNKS
        state = pltpu.VMEM((6, CHUNKS, width, step), jnp.float32)
        copies = pltpu.SemaphoreType.DMA
        return pl.pallas_call(
            functools.partial(kernel, pairs, rows),
            out_shape=jax.ShapeDtypeStruct(snapshots.shape, jnp.float32),
            in_specs=[
                pl.BlockSpec(memory_space=pltpu.SMEM),
                pl.BlockSpec(memory_space=pltpu.HBM),
            ],
            out_specs=pl.BlockSpec(memory_space=pltpu.VMEM),
            scratch_shapes=[
                pltpu.VMEM((full, cells), jnp.float32),
                pltpu.VMEM((CHUNKS, full, step), jnp.float32),
                state,
                state,
                state,
                pltpu.VMEM((AHEAD, 2, width, step), jnp.float32),
                pltpu.VMEM((2, CHUNKS, width, step), jnp.float32),
                pltpu.VMEM((2, RAW_ONE, 2, width, step), jnp.float32),
                pltpu.VMEM((2, RAW_TWO, 2, width, step), jnp.float32),
                pltpu.VMEM((2, 2, width, full), jnp.float32),
                pltpu.VMEM((2, 2, width, full), jnp.float32),
                pltpu.VMEM((rows, width // 2 + 8, full), jnp.float32),
                pltpu.VMEM((2, 2 * rows, width + 8, full), jnp.float32),
                pltpu.VMEM((2 * rows, width // 2 + 8, full), jnp.float32),
                pltpu.VMEM((4, width // 2 + 8, full), jnp.float32),
                copies((CHUNKS,)),
                copies((CHUNKS,)),
                copies((CHUNKS,)),
                copies((2,)),
                copies((rows,)),
                copies((rows,)),
                copies((2, 2 * rows)),
                copies((2, 2 * rows)),
                copies((2 * rows,)),
                copies((2 * rows,)),
                copies((3, 2, CHUNKS)),
                copies((3, 2, CHUNKS)),
                copies((AHEAD,)),
                copies((AHEAD,)),
                copies((2, CHUNKS)),
                copies((2, CHUNKS)),
                copies((2, 2, CHUNKS)),
                copies((2, 2, CHUNKS)),
                copies((2, 2)),
                copies((2, 2)),
            ],
            compiler_params=pltpu.CompilerParams(
                collective_id=0, has_side_effects=True, vmem_limit_bytes=48 * 1024 * 1024
            ),
        )(live_rows, pltpu.with_memory_space_constraint(snapshots, pltpu.HBM))

    return jax.shard_map(
        body,
        mesh=mesh,
        in_specs=(P("pair", "row"), P("row")),
        out_specs=P("pair", "row"),
        check_vma=False,
    )
```
